32 devices in a mesh: group: 4 (over y, x), brick: 8 (over z, core).
Axes of the slice: x: 2, y: 2, z: 4, core: 2. Of those that a mesh axis runs over, the one named last changes fastest.
Arguments:
- populations: float32 [19, 8, 64, 128], P(None, 'group', 'brick'), may hold values from 0 to 1, as said below
- positions: float32 [3, 64, 642], P(None, ('group', 'brick')), may hold values from -6 to 6
- rest_shape: float32 [3, 642], replicated, may hold values from -6 to 6
- inverse: float32 [642, 642], replicated, may hold values from -2 to 2, as said below
- sample_cells: int32 [32, 64], P(('group', 'brick')), may hold values from 0 to 2047
- vertex_slots: int32 [32, 1284], P(('group', 'brick')), may hold values from 0 to 63, as said below
- pair_own: int32 [32, 2048], P(('group', 'brick')), may hold values from 0 to 1283
- pair_far: int32 [32, 2048], P(('group', 'brick')), may hold values from 0 to 1283
Outputs:
- new_populations: float32 [19, 8, 64, 128], P(None, 'group', 'brick')
- new_positions: float32 [3, 64, 642], P(None, ('group', 'brick'))
The draws below stay inside these ranges and needn't reach their ends.
Inputs may be any that keep to these rules, and one draw needn't show every extreme that they name: Every population is positive and a cell's populations sum to between 0.6 and 1.4. inverse is symmetric. `vertex_slots`: on every device each slot 0 to 63 is named by at least one vertex.
All inputs are finite; a program needn't handle non-finite values.
Results may differ from the reference program's by a relative error of at most 0.0001.
Values sent between devices are 32-bit elements; how exact they have to be, the bound alone decides.
A program may use at most 64 MiB of HBM per device.

```python
import jax
import jax.numpy as jnp
from jax import lax

V = 642
B_DEV = 2
CX = 2
CY = 8
NZ = 128
C_PEER = 8
NPAIR = 2048
ITERS = 4
STEPS = 2
NX = 8
NY = 64
SLOTS = 64
BODIES = 64
N_GROUP = 4
N_BRICK = 8


weights_table = [1.0 / 3.0] + [1.0 / 18.0] * 6 + [1.0 / 36.0] * 12


def draw_populations(key, part):
    weight_col = jnp.array(weights_table, jnp.float32)[:, None, None, None]
    dims = (19, NX, NY, NZ)
    factor = 1.0 + jnp.clip(0.15 * jax.random.normal(key, dims, jnp.float32), -0.4, 0.4)
    return weight_col * factor


def draw_inverse(key, part):
    noise = jax.random.normal(key, (V, V), jnp.float32)
    noise = noise / jnp.sqrt(jnp.float32(V))
    symmetric = (noise + noise.T) * 0.7071
    return 0.5 * (jnp.eye(V, dtype=jnp.float32) + 0.25 * symmetric)


def draw_vertex_slots(key, part):
    keys = jax.random.split(jax.random.fold_in(key, 7), N_GROUP * N_BRICK)
    orders = jax.vmap(lambda single: jax.random.permutation(single, B_DEV * V))(keys)
    return (orders % (C_PEER * N_BRICK)).astype(jnp.int32)


def place_ends(drawn, stream_key, smallest, top_value):
    index_at = [jax.random.randint(jax.random.fold_in(stream_key, axis), (), 0, length) for axis, length in enumerate(drawn.shape)]
    longest = drawn.shape.index(max(drawn.shape))
    beside = index_at[:longest] + [(index_at[longest] + 1) % drawn.shape[longest]] + index_at[longest + 1:]
    return drawn.at[tuple(index_at)].set(smallest).at[tuple(beside)].set(top_value)


def block_levels(key, shape, pieces, least, largest):
    level = 1.0
    for axis_at, blocks in pieces:
        steps = jax.random.uniform(jax.random.fold_in(jax.random.fold_in(key, 6), axis_at), (blocks,), jnp.float32, least / len(pieces), largest / len(pieces))
        level = level * jnp.repeat(jnp.exp(steps), shape[axis_at] // blocks).reshape((-1,) + (1,) * (len(shape) - 1 - axis_at))
    return level


def bell_draw(key, extent, width, reach, shards=(), kind=jnp.bfloat16):
    factor_of = block_levels(key, extent, shards, -0.22, 0.18) if shards else 1.0
    drawn = jax.random.normal(key, extent, jnp.float32) * width * factor_of
    return jnp.minimum(jnp.maximum(drawn, -reach), reach).astype(kind)


def setup_inputs(seed: int = 0) -> dict:
    splits = jax.random.split(jax.random.key(seed), 9)
    return {
        "populations": draw_populations(jax.random.fold_in(splits[8], 71), 0),
        "positions": bell_draw(splits[1], (3, BODIES, V), 1.0, 6.0, ((1, 32),), jnp.float32),
        "rest_shape": bell_draw(splits[2], (3, V), 1.0, 6.0, (), jnp.float32),
        "inverse": draw_inverse(jax.random.fold_in(splits[8], 71), 0),
        "sample_cells": place_ends(jax.random.randint(splits[4], (N_GROUP * N_BRICK, SLOTS), 0, CX * CY * NZ), jax.random.fold_in(splits[4], 1), 0, (CX * CY * NZ) - 1).astype(jnp.int32),
        "vertex_slots": draw_vertex_slots(jax.random.fold_in(splits[8], 71), 0),
        "pair_own": place_ends(jax.random.randint(splits[6], (N_GROUP * N_BRICK, NPAIR), 0, B_DEV * V), jax.random.fold_in(splits[6], 1), 0, (B_DEV * V) - 1).astype(jnp.int32),
        "pair_far": place_ends(jax.random.randint(splits[7], (N_GROUP * N_BRICK, NPAIR), 0, B_DEV * V), jax.random.fold_in(splits[7], 1), 0, (B_DEV * V) - 1).astype(jnp.int32),
    }


velocities = [(0, 0, 0), (0, 0, 1), (0, 0, -1), (1, 0, 0), (-1, 0, 0), (0, 1, 0), (0, -1, 0),
              (1, 1, 0), (-1, -1, 0), (1, -1, 0), (-1, 1, 0), (1, 0, 1), (-1, 0, -1), (1, 0, -1),
              (-1, 0, 1), (0, 1, 1), (0, -1, -1), (0, 1, -1), (0, -1, 1)]
weights_table = [1.0 / 3.0] + [1.0 / 18.0] * 6 + [1.0 / 36.0] * 12
relax_time = 0.8
contact_gain = 0.5
contact_range = 6.0
coupling_gain = 0.05
mass_weight = 1.0
shape_weight = 1.0
time_step = 1.0


def moments(populations):
    table = jnp.array(velocities, jnp.float32)
    density = jnp.sum(populations, axis=0)
    momentum = jnp.einsum("iq,ixyz->qxyz", table, populations, precision=lax.Precision.HIGHEST)
    return density, momentum


def collide(populations, force):
    table = jnp.array(velocities, jnp.float32)
    weight_col = jnp.array(weights_table, jnp.float32)[:, None, None, None]
    density, momentum = moments(populations)
    veloc = (momentum + 0.5 * force) / density
    project = jnp.einsum("iq,qxyz->ixyz", table, veloc, precision=lax.Precision.HIGHEST)
    forcing = jnp.einsum("iq,qxyz->ixyz", table, force, precision=lax.Precision.HIGHEST)
    square = jnp.sum(veloc * veloc, axis=0)
    equil = weight_col * density * (1.0 + 3.0 * project + 4.5 * project * project - 1.5 * square)
    return populations - (populations - equil) / relax_time + 3.0 * weight_col * forcing


def stream(post):
    moved = [jnp.roll(post[index], velocities[index], axis=(0, 1, 2)) for index in range(19)]
    return jnp.stack(moved, axis=0)


def to_blocks(field):
    parts = field.reshape(3, N_GROUP, CX, N_BRICK, CY, NZ).transpose(0, 1, 3, 2, 4, 5)
    return parts.reshape(3, N_GROUP, N_BRICK, CX * CY * NZ)


def from_blocks(blocks):
    parts = blocks.reshape(3, N_GROUP, N_BRICK, CX, CY, NZ).transpose(0, 1, 3, 2, 4, 5)
    return parts.reshape(3, N_GROUP * CX, N_BRICK * CY, NZ)


def add_rows(values, index, count):
    return jnp.zeros((3, count), jnp.float32).at[:, index].add(values)


def reference(populations, positions, rest_shape, inverse, sample_cells, vertex_slots, pair_own, pair_far):
    devices = N_GROUP * N_BRICK
    cells = CX * CY * NZ
    verts = B_DEV * V
    slot_count = C_PEER * N_BRICK
    dist = populations
    shape = positions.reshape(3, devices, verts)
    request = sample_cells.reshape(N_GROUP, N_BRICK, slot_count)
    for step_index in range(STEPS):
        density, momentum = moments(dist)
        flow = momentum / density
        picked = jnp.take_along_axis(to_blocks(flow), request[None], axis=3)
        received = picked.reshape(3, N_GROUP, N_BRICK, N_BRICK, C_PEER).transpose(0, 1, 3, 2, 4)
        received = received.reshape(3, devices, slot_count)
        vertex_flow = jnp.take_along_axis(received, vertex_slots[None], axis=2)
        predicted = shape + time_step * vertex_flow
        for sweep_index in range(ITERS):
            lower = jnp.roll(shape.reshape(3, N_GROUP, N_BRICK, verts), 1, axis=2).reshape(3, devices, verts)
            own_points = jnp.take_along_axis(shape, pair_own[None], axis=2)
            far_points = jnp.take_along_axis(lower, pair_far[None], axis=2)
            diff = own_points - far_points
            weight = jnp.exp(-jnp.sum(diff * diff, axis=0) / contact_range)
            push = contact_gain * weight * diff
            contact = jax.vmap(lambda values, index: add_rows(values, index, verts), in_axes=(1, 0), out_axes=1)(push, pair_own)
            bodies = shape.reshape(3, devices, B_DEV, V)
            centroid = jnp.mean(bodies, axis=3, keepdims=True)
            target = (centroid + rest_shape[:, None, None, :]).reshape(3, devices, verts)
            rhs = mass_weight * predicted + shape_weight * target + contact
            shape = jnp.dot(rhs.reshape(3 * devices * B_DEV, V), inverse,
                            precision=lax.Precision.HIGHEST, preferred_element_type=jnp.float32).reshape(3, devices, verts)
        vertex_force = coupling_gain * (shape - predicted)
        slot_force = jax.vmap(lambda values, index: add_rows(values, index, slot_count), in_axes=(1, 0), out_axes=1)(vertex_force, vertex_slots)
        back = slot_force.reshape(3, N_GROUP, N_BRICK, N_BRICK, C_PEER).transpose(0, 1, 3, 2, 4)
        back = back.reshape(3, devices, slot_count)
        cell_force = jax.vmap(lambda values, index: add_rows(values, index, cells), in_axes=(1, 0), out_axes=1)(back, sample_cells)
        force = from_blocks(cell_force.reshape(3, N_GROUP, N_BRICK, cells))
        dist = stream(collide(dist, force))
    return dist, shape.reshape(3, devices * B_DEV, V)
```

```python
import functools

import jax
import jax.numpy as jnp
from jax import lax
from jax.experimental import pallas as pl
from jax.experimental.pallas import tpu as pltpu
from jax.sharding import PartitionSpec as P

ITERS = 4
STEPS = 2


velocities = [
    (0, 0, 0),
    (0, 0, 1),
    (0, 0, -1),
    (1, 0, 0),
    (-1, 0, 0),
    (0, 1, 0),
    (0, -1, 0),
    (1, 1, 0),
    (-1, -1, 0),
    (1, -1, 0),
    (-1, 1, 0),
    (1, 0, 1),
    (-1, 0, -1),
    (1, 0, -1),
    (-1, 0, 1),
    (0, 1, 1),
    (0, -1, -1),
    (0, 1, -1),
    (0, -1, 1),
]
weights_table = [1.0 / 3.0] + [1.0 / 18.0] * 6 + [1.0 / 36.0] * 12
relax_time = 0.8
contact_gain = 0.5
contact_range = 6.0
coupling_gain = 0.05
mass_weight = 1.0
shape_weight = 1.0
time_step = 1.0


def extended(cells, sides, width):
    for axis, dim in sides:
        count = lax.axis_size(axis)
        head = lax.slice_in_dim(cells, 0, width, axis=dim)
        tail = lax.slice_in_dim(cells, cells.shape[dim] - width, cells.shape[dim], axis=dim)
        cells = jnp.concatenate(
            [
                lax.ppermute(tail, axis, [(i, (i + 1) % count) for i in range(count)]),
                cells,
                lax.ppermute(head, axis, [((i + 1) % count, i) for i in range(count)]),
            ],
            axis=dim,
        )
    return cells


def shifted_2(array, axis, by):
    peers = lax.axis_size(axis)
    return lax.ppermute(array, axis, [(i, (i + by) % peers) for i in range(peers)])


def moments(populations):
    table = jnp.array(velocities, jnp.float32)
    density = jnp.sum(populations, axis=0)
    momentum = jnp.einsum("iq,ixyz->qxyz", table, populations, precision=lax.Precision.HIGHEST)
    return (density, momentum)


def collide(populations, force):
    table = jnp.array(velocities, jnp.float32)
    weight_col = jnp.array(weights_table, jnp.float32)[:, None, None, None]
    density, momentum = moments(populations)
    veloc = (momentum + 0.5 * force) / density
    project = jnp.einsum("iq,qxyz->ixyz", table, veloc, precision=lax.Precision.HIGHEST)
    forcing = jnp.einsum("iq,qxyz->ixyz", table, force, precision=lax.Precision.HIGHEST)
    square = jnp.sum(veloc * veloc, axis=0)
    equil = weight_col * density * (1.0 + 3.0 * project + 4.5 * project * project - 1.5 * square)
    return populations - (populations - equil) / relax_time + 3.0 * weight_col * forcing


def shifted(padded, index, width_x, width_y):
    step_x, step_y, step_z = velocities[index]
    piece = padded[1 - step_x : 1 - step_x + width_x, 1 - step_y : 1 - step_y + width_y, :]
    return jnp.roll(piece, step_z, axis=2)


def stream(post):
    width_x, width_y = (post.shape[1], post.shape[2])
    padded = extended(post, (("group", 1), ("brick", 2)), 1)
    moved = [shifted(padded[index], index, width_x, width_y) for index in range(19)]
    return jnp.stack(moved, axis=0)


LANES = 128
BODY_ROWS = 4


def pieces(value):
    high = value.astype(jnp.bfloat16)
    rest = value - high.astype(jnp.float32)
    middle = rest.astype(jnp.bfloat16)
    low = (rest - middle.astype(jnp.float32)).astype(jnp.bfloat16)
    return high, middle, low


def pick(points, hot, block, body):
    rows, width = points.shape
    blocks = width // LANES
    table = jnp.concatenate([points[:, h * LANES : (h + 1) * LANES] for h in range(blocks)], axis=0)
    got = jnp.dot(jnp.concatenate(pieces(table), axis=0), hot, preferred_element_type=jnp.float32)
    size = rows * blocks
    got = got[:size] + got[size : 2 * size] + got[2 * size :]
    total = jnp.zeros((rows, hot.shape[1]), jnp.float32)
    for h in range(blocks):
        total = total + jnp.where(block == h, got[h * rows : (h + 1) * rows], 0.0)
    row_body = lax.broadcasted_iota(jnp.int32, total.shape, 0) // BODY_ROWS
    total = jnp.where(row_body == body, total, 0.0)
    out = total
    for k in range(1, rows // BODY_ROWS):
        out = out + pltpu.roll(total, k * BODY_ROWS, 0)
    return out


def bodies_kernel(
    count, verts, shape_ref, predicted_ref, rest_ref, high_ref, middle_ref, index_ref, out_ref,
    own_hot, far_hot, current, lower, send_sem, recv_sem,
):
    me = lax.axis_index("brick")
    group = lax.axis_index("group")
    above = lax.rem(me + 1, count)
    below = lax.rem(me + count - 1, count)
    barrier = pltpu.get_barrier_semaphore()
    pl.semaphore_signal(barrier, inc=1, device_id=(group, below), device_id_type=pl.DeviceIdType.MESH)
    pl.semaphore_wait(barrier, 1)
    rows, width = shape_ref.shape
    blocks = width // LANES
    bodies = rows // BODY_ROWS
    pairs = index_ref.shape[1]
    copies = []

    def send(source, slot):
        copy = pltpu.make_async_remote_copy(
            src_ref=source,
            dst_ref=lower.at[slot],
            send_sem=send_sem.at[slot],
            recv_sem=recv_sem.at[slot],
            device_id=(group, above),
            device_id_type=pl.DeviceIdType.MESH,
        )
        copy.start()
        copies.append(copy)

    send(shape_ref, 0)
    lane = lax.broadcasted_iota(jnp.int32, (LANES, pairs), 0)
    own_hot[...] = jnp.where(lane == index_ref[0:1, :], 1.0, 0.0).astype(jnp.bfloat16)
    far_hot[...] = jnp.where(lane == index_ref[3:4, :], 1.0, 0.0).astype(jnp.bfloat16)
    own_block, own_body = index_ref[1:2, :], index_ref[2:3, :]
    far_block, far_body = index_ref[4:5, :], index_ref[5:6, :]
    row_body = lax.broadcasted_iota(jnp.int32, (rows, pairs), 0) // BODY_ROWS
    for sweep in range(ITERS):
        shape = shape_ref[...] if sweep == 0 else current[sweep]
        own = pick(shape, own_hot[...], own_block, own_body)
        centroid = jnp.sum(shape, axis=1, keepdims=True) * (1.0 / verts)
        base = mass_weight * predicted_ref[...] + shape_weight * (centroid + rest_ref[...])
        copies[sweep].wait_recv()
        far = pick(lower[sweep], far_hot[...], far_block, far_body)
        diff = own - far
        square = jnp.sum(diff * diff, axis=0, keepdims=True) * (1.0 / bodies)
        push = contact_gain * jnp.exp(square * (-1.0 / contact_range)) * diff
        push = jnp.where(row_body == own_body, push, 0.0)
        parts = [
            jnp.concatenate(
                [jnp.where(own_block == h, part.astype(jnp.float32), 0.0) for h in range(blocks)], axis=0
            ).astype(jnp.bfloat16)
            for part in pieces(push)
        ]
        added = lax.dot_general(
            jnp.concatenate(parts, axis=0), own_hot[...], (((1,), (1,)), ((), ())),
            preferred_element_type=jnp.float32,
        )
        size = rows * blocks
        added = added[:size] + added[size : 2 * size] + added[2 * size :]
        contact = jnp.concatenate([added[h * rows : (h + 1) * rows] for h in range(blocks)], axis=1)
        rhs = base + contact
        split = jnp.concatenate([part.astype(jnp.float32) for part in pieces(rhs)], axis=0).astype(jnp.bfloat16)
        by_high = jnp.dot(split, high_ref[...], preferred_element_type=jnp.float32)
        by_middle = jnp.dot(split, middle_ref[...], preferred_element_type=jnp.float32)
        both = by_high + by_middle
        shape = both[:rows] + both[rows : 2 * rows] + both[2 * rows :]
        if sweep < ITERS - 1:
            current[sweep + 1] = shape
            send(current.at[sweep + 1], sweep + 1)
        else:
            out_ref[...] = shape
    for copy in copies:
        copy.wait_send()


def run_bodies(verts, shape, predicted, rest, high, middle, index):
    rows, width = shape.shape
    pairs = index.shape[1]
    return pl.pallas_call(
        functools.partial(bodies_kernel, lax.axis_size("brick"), verts),
        out_shape=jax.ShapeDtypeStruct((rows, width), jnp.float32),
        in_specs=[pl.BlockSpec(memory_space=pltpu.VMEM)] * 6,
        out_specs=pl.BlockSpec(memory_space=pltpu.VMEM),
        scratch_shapes=[
            pltpu.VMEM((LANES, pairs), jnp.bfloat16),
            pltpu.VMEM((LANES, pairs), jnp.bfloat16),
            pltpu.VMEM((ITERS, rows, width), jnp.float32),
            pltpu.VMEM((ITERS, rows, width), jnp.float32),
            pltpu.SemaphoreType.DMA((ITERS,)),
            pltpu.SemaphoreType.DMA((ITERS,)),
        ],
        compiler_params=pltpu.CompilerParams(collective_id=0, has_side_effects=True),
    )(shape, predicted, rest, high, middle, index)


def on_device(
    populations, positions, rest_shape, inverse, sample_cells, vertex_slots, pair_own, pair_far
):
    exact = lax.Precision.HIGHEST
    brick_count = lax.axis_size("brick")
    slot_count = sample_cells.shape[1]
    peer_count = slot_count // brick_count
    bodies, verts = positions.shape[1:]
    width = -(-verts // LANES) * LANES
    pad = width - verts
    grid_shape = populations.shape[1:]
    lanes = grid_shape[2]
    lines = grid_shape[0] * grid_shape[1]

    def to_rows(value):
        return jnp.pad(value.transpose(1, 0, 2), ((0, 0), (0, 1), (0, pad))).reshape(bodies * BODY_ROWS, width)

    def from_rows(value):
        return value.reshape(bodies, BODY_ROWS, width)[:, :3, :verts].transpose(1, 0, 2)

    request = sample_cells[0]
    cell_lane = (request[None, :] % lanes == jnp.arange(lanes)[:, None]).astype(jnp.float32)
    cell_line = (request[None, :] // lanes == jnp.arange(lines)[:, None]).astype(jnp.float32)
    slots = jnp.pad(vertex_slots.reshape(bodies, verts), ((0, 0), (0, pad)), constant_values=-1)
    slot_hot = (slots[:, None, :] == jnp.arange(slot_count)[None, :, None]).astype(jnp.float32)

    def places(index):
        body, vertex = index // verts, index % verts
        return [vertex % LANES, vertex // LANES, body]

    index = jnp.stack(places(pair_own[0]) + places(pair_far[0]) + [pair_own[0]] * 2, axis=0)
    full = jnp.pad(inverse, ((0, pad), (0, pad)))
    high = lax.reduce_precision(full, 8, 7)
    middle = (full - high).astype(jnp.bfloat16)
    high = high.astype(jnp.bfloat16)
    rest = to_rows(jnp.broadcast_to(rest_shape[:, None, :], positions.shape))
    dist = populations
    shape = to_rows(positions)
    for step_index in range(STEPS):
        density, momentum = moments(dist)
        flow = (momentum / density).reshape(3, lines, lanes)
        outgoing = jnp.einsum("cxl,lk->cxk", flow, cell_lane, precision=exact)
        outgoing = jnp.sum(outgoing * cell_line[None], axis=1)
        received = lax.all_to_all(
            outgoing.reshape(3, brick_count, peer_count), "brick", split_axis=1, concat_axis=1, tiled=True
        ).reshape(3, slot_count)
        received = jnp.pad(received, ((0, 1), (0, 0)))
        vertex_flow = jnp.einsum("cs,bsv->bcv", received, slot_hot, precision=exact)
        predicted = shape + time_step * vertex_flow.reshape(shape.shape)
        shape = run_bodies(verts, shape, predicted, rest, high, middle, index)
        vertex_force = (coupling_gain * (shape - predicted)).reshape(bodies, BODY_ROWS, width)
        slot_force = jnp.einsum("bcv,bsv->cs", vertex_force, slot_hot, precision=exact)[:3]
        back = lax.all_to_all(
            slot_force.reshape(3, brick_count, peer_count), "brick", split_axis=1, concat_axis=1, tiled=True
        ).reshape(3, slot_count)
        cell_force = jnp.einsum("cxk,lk->cxl", back[:, None, :] * cell_line[None], cell_lane, precision=exact)
        force = cell_force.reshape((3,) + grid_shape)
        dist = stream(collide(dist, force))
    return (dist, from_rows(shape))


def solution(mesh):
    placed = (
        P(None, "group", "brick", None),
        P(None, ("group", "brick"), None),
        P(),
        P(),
        P(("group", "brick"), None),
        P(("group", "brick"), None),
        P(("group", "brick"), None),
        P(("group", "brick"), None),
    )
    return jax.shard_map(
        on_device,
        mesh=mesh,
        in_specs=placed,
        out_specs=(P(None, "group", "brick", None), P(None, ("group", "brick"), None)),
        check_vma=False,
    )
```

```python
import functools

import jax
import jax.numpy as jnp
from jax import lax
from jax.experimental import pallas as pl
from jax.experimental.pallas import tpu as pltpu
from jax.sharding import PartitionSpec as P

ITERS = 4
STEPS = 2


velocities = [
    (0, 0, 0),
    (0, 0, 1),
    (0, 0, -1),
    (1, 0, 0),
    (-1, 0, 0),
    (0, 1, 0),
    (0, -1, 0),
    (1, 1, 0),
    (-1, -1, 0),
    (1, -1, 0),
    (-1, 1, 0),
    (1, 0, 1),
    (-1, 0, -1),
    (1, 0, -1),
    (-1, 0, 1),
    (0, 1, 1),
    (0, -1, -1),
    (0, 1, -1),
    (0, -1, 1),
]
weights_table = [1.0 / 3.0] + [1.0 / 18.0] * 6 + [1.0 / 36.0] * 12
relax_time = 0.8
contact_gain = 0.5
contact_range = 6.0
coupling_gain = 0.05
mass_weight = 1.0
shape_weight = 1.0
time_step = 1.0


def extended(cells, sides, width):
    for axis, dim in sides:
        count = lax.axis_size(axis)
        head = lax.slice_in_dim(cells, 0, width, axis=dim)
        tail = lax.slice_in_dim(cells, cells.shape[dim] - width, cells.shape[dim], axis=dim)
        cells = jnp.concatenate(
            [
                lax.ppermute(tail, axis, [(i, (i + 1) % count) for i in range(count)]),
                cells,
                lax.ppermute(head, axis, [((i + 1) % count, i) for i in range(count)]),
            ],
            axis=dim,
        )
    return cells


def shifted_2(array, axis, by):
    peers = lax.axis_size(axis)
    return lax.ppermute(array, axis, [(i, (i + by) % peers) for i in range(peers)])


def moments(populations):
    table = jnp.array(velocities, jnp.float32)
    density = jnp.sum(populations, axis=0)
    momentum = jnp.einsum("iq,ixyz->qxyz", table, populations, precision=lax.Precision.HIGHEST)
    return (density, momentum)


def collide(populations, force):
    table = jnp.array(velocities, jnp.float32)
    weight_col = jnp.array(weights_table, jnp.float32)[:, None, None, None]
    density, momentum = moments(populations)
    veloc = (momentum + 0.5 * force) / density
    project = jnp.einsum("iq,qxyz->ixyz", table, veloc, precision=lax.Precision.HIGHEST)
    forcing = jnp.einsum("iq,qxyz->ixyz", table, force, precision=lax.Precision.HIGHEST)
    square = jnp.sum(veloc * veloc, axis=0)
    equil = weight_col * density * (1.0 + 3.0 * project + 4.5 * project * project - 1.5 * square)
    return populations - (populations - equil) / relax_time + 3.0 * weight_col * forcing


def shifted(padded, index, width_x, width_y):
    step_x, step_y, step_z = velocities[index]
    piece = padded[1 - step_x : 1 - step_x + width_x, 1 - step_y : 1 - step_y + width_y, :]
    return jnp.roll(piece, step_z, axis=2)


def stream(post):
    width_x, width_y = (post.shape[1], post.shape[2])
    padded = extended(post, (("group", 1), ("brick", 2)), 1)
    moved = [shifted(padded[index], index, width_x, width_y) for index in range(19)]
    return jnp.stack(moved, axis=0)


LANES = 128
BODY_ROWS = 4


def pieces(value):
    high = value.astype(jnp.bfloat16)
    rest = value - high.astype(jnp.float32)
    middle = rest.astype(jnp.bfloat16)
    low = (rest - middle.astype(jnp.float32)).astype(jnp.bfloat16)
    return high, middle, low


def pick(points, hot, block, body):
    rows, width = points.shape
    blocks = width // LANES
    table = jnp.concatenate([points[:, h * LANES : (h + 1) * LANES] for h in range(blocks)], axis=0)
    got = jnp.dot(jnp.concatenate(pieces(table), axis=0), hot, preferred_element_type=jnp.float32)
    size = rows * blocks
    got = got[:size] + got[size : 2 * size] + got[2 * size :]
    total = jnp.zeros((rows, hot.shape[1]), jnp.float32)
    for h in range(blocks):
        total = total + jnp.where(block == h, got[h * rows : (h + 1) * rows], 0.0)
    row_body = lax.broadcasted_iota(jnp.int32, total.shape, 0) // BODY_ROWS
    total = jnp.where(row_body == body, total, 0.0)
    out = total
    for k in range(1, rows // BODY_ROWS):
        out = out + pltpu.roll(total, k * BODY_ROWS, 0)
    return out


def bodies_kernel(
    count, verts, shape_ref, predicted_ref, rest_ref, high_ref, middle_ref, index_ref, out_ref,
    own_hot, far_hot, current, lower, send_sem, recv_sem,
):
    me = lax.axis_index("brick")
    group = lax.axis_index("group")
    above = lax.rem(me + 1, count)
    below = lax.rem(me + count - 1, count)
    barrier = pltpu.get_barrier_semaphore()
    pl.semaphore_signal(barrier, inc=1, device_id=(group, below), device_id_type=pl.DeviceIdType.MESH)
    pl.semaphore_wait(barrier, 1)
    rows, width = shape_ref.shape
    blocks = width // LANES
    bodies = rows // BODY_ROWS
    pairs = index_ref.shape[1]
    copies = []

    def send(source, slot):
        copy = pltpu.make_async_remote_copy(
            src_ref=source,
            dst_ref=lower.at[slot],
            send_sem=send_sem.at[slot],
            recv_sem=recv_sem.at[slot],
            device_id=(group, above),
            device_id_type=pl.DeviceIdType.MESH,
        )
        copy.start()
        copies.append(copy)

    send(shape_ref, 0)
    lane = lax.broadcasted_iota(jnp.int32, (LANES, pairs), 0)
    own_hot[...] = jnp.where(lane == index_ref[0:1, :], 1.0, 0.0).astype(jnp.bfloat16)
    far_hot[...] = jnp.where(lane == index_ref[3:4, :], 1.0, 0.0).astype(jnp.bfloat16)
    own_block, own_body = index_ref[1:2, :], index_ref[2:3, :]
    far_block, far_body = index_ref[4:5, :], index_ref[5:6, :]
    row_body = lax.broadcasted_iota(jnp.int32, (rows, pairs), 0) // BODY_ROWS
    for sweep in range(ITERS):
        shape = shape_ref[...] if sweep == 0 else current[sweep]
        own = pick(shape, own_hot[...], own_block, own_body)
        centroid = jnp.sum(shape, axis=1, keepdims=True) * (1.0 / verts)
        base = mass_weight * predicted_ref[...] + shape_weight * (centroid + rest_ref[...])
        copies[sweep].wait_recv()
        far = pick(lower[sweep], far_hot[...], far_block, far_body)
        diff = own - far
        square = jnp.sum(diff * diff, axis=0, keepdims=True) * (1.0 / bodies)
        push = contact_gain * jnp.exp(square * (-1.0 / contact_range)) * diff
        push = jnp.where(row_body == own_body, push, 0.0)
        parts = [
            jnp.concatenate(
                [jnp.where(own_block == h, part.astype(jnp.float32), 0.0) for h in range(blocks)], axis=0
            ).astype(jnp.bfloat16)
            for part in pieces(push)
        ]
        added = lax.dot_general(
            jnp.concatenate(parts, axis=0), own_hot[...], (((1,), (1,)), ((), ())),
            preferred_element_type=jnp.float32,
        )
        size = rows * blocks
        added = added[:size] + added[size : 2 * size] + added[2 * size :]
        contact = jnp.concatenate([added[h * rows : (h + 1) * rows] for h in range(blocks)], axis=1)
        rhs = base + contact
        split = jnp.concatenate([part.astype(jnp.float32) for part in pieces(rhs)], axis=0).astype(jnp.bfloat16)
        by_high = jnp.dot(split, high_ref[...], preferred_element_type=jnp.float32)
        by_middle = jnp.dot(split, middle_ref[...], preferred_element_type=jnp.float32)
        both = by_high + by_middle
        shape = both[:rows] + both[rows : 2 * rows] + both[2 * rows :]
        if sweep < ITERS - 1:
            current[sweep + 1] = shape
            send(current.at[sweep + 1], sweep + 1)
        else:
            out_ref[...] = shape
    for copy in copies:
        copy.wait_send()


def run_bodies(verts, shape, predicted, rest, high, middle, index):
    rows, width = shape.shape
    pairs = index.shape[1]
    return pl.pallas_call(
        functools.partial(bodies_kernel, lax.axis_size("brick"), verts),
        out_shape=jax.ShapeDtypeStruct((rows, width), jnp.float32),
        in_specs=[pl.BlockSpec(memory_space=pltpu.VMEM)] * 6,
        out_specs=pl.BlockSpec(memory_space=pltpu.VMEM),
        scratch_shapes=[
            pltpu.VMEM((LANES, pairs), jnp.bfloat16),
            pltpu.VMEM((LANES, pairs), jnp.bfloat16),
            pltpu.VMEM((ITERS, rows, width), jnp.float32),
            pltpu.VMEM((ITERS, rows, width), jnp.float32),
            pltpu.SemaphoreType.DMA((ITERS,)),
            pltpu.SemaphoreType.DMA((ITERS,)),
        ],
        compiler_params=pltpu.CompilerParams(collective_id=0, has_side_effects=True),
    )(shape, predicted, rest, high, middle, index)


def swap_kernel(count, blocks_ref, out_ref, local_sem, send_sem, recv_sem):
    me = lax.axis_index("brick")
    group = lax.axis_index("group")
    barrier = pltpu.get_barrier_semaphore()

    def copy_to(step):
        peer = lax.rem(me + step, count)
        return peer, pltpu.make_async_remote_copy(
            src_ref=blocks_ref.at[peer],
            dst_ref=out_ref.at[me],
            send_sem=send_sem.at[step],
            recv_sem=recv_sem.at[step],
            device_id=(group, peer),
            device_id_type=pl.DeviceIdType.MESH,
        )

    @pl.loop(1, count)
    def _(step):
        peer = lax.rem(me + step, count)
        pl.semaphore_signal(barrier, inc=1, device_id=(group, peer), device_id_type=pl.DeviceIdType.MESH)

    own = pltpu.make_async_copy(blocks_ref.at[me], out_ref.at[me], local_sem)
    own.start()
    pl.semaphore_wait(barrier, count - 1)

    @pl.loop(1, count)
    def _(step):
        copy_to(step)[1].start()

    own.wait()

    @pl.loop(1, count)
    def _(step):
        copy_to(step)[1].wait()


def swap(value):
    count = lax.axis_size("brick")
    each = value.shape[1] // count
    blocks = value.reshape(3, count, each).transpose(1, 0, 2)
    blocks = jnp.pad(blocks, ((0, 0), (0, 5), (0, LANES - each)))
    blocks = pl.pallas_call(
        functools.partial(swap_kernel, count),
        out_shape=jax.ShapeDtypeStruct(blocks.shape, jnp.float32),
        in_specs=[pl.BlockSpec(memory_space=pltpu.VMEM)],
        out_specs=pl.BlockSpec(memory_space=pltpu.VMEM),
        scratch_shapes=[
            pltpu.SemaphoreType.DMA,
            pltpu.SemaphoreType.DMA((count,)),
            pltpu.SemaphoreType.DMA((count,)),
        ],
        compiler_params=pltpu.CompilerParams(collective_id=1, has_side_effects=True),
    )(blocks)
    return blocks[:, :3, :each].transpose(1, 0, 2).reshape(value.shape)


def on_device(
    populations, positions, rest_shape, inverse, sample_cells, vertex_slots, pair_own, pair_far
):
    exact = lax.Precision.HIGHEST
    slot_count = sample_cells.shape[1]
    bodies, verts = positions.shape[1:]
    width = -(-verts // LANES) * LANES
    pad = width - verts
    grid_shape = populations.shape[1:]
    lanes = grid_shape[2]
    lines = grid_shape[0] * grid_shape[1]

    def to_rows(value):
        return jnp.pad(value.transpose(1, 0, 2), ((0, 0), (0, 1), (0, pad))).reshape(bodies * BODY_ROWS, width)

    def from_rows(value):
        return value.reshape(bodies, BODY_ROWS, width)[:, :3, :verts].transpose(1, 0, 2)

    request = sample_cells[0]
    cell_lane = (request[None, :] % lanes == jnp.arange(lanes)[:, None]).astype(jnp.float32)
    cell_line = (request[None, :] // lanes == jnp.arange(lines)[:, None]).astype(jnp.float32)
    slots = jnp.pad(vertex_slots.reshape(bodies, verts), ((0, 0), (0, pad)), constant_values=-1)
    slot_hot = (slots[:, None, :] == jnp.arange(slot_count)[None, :, None]).astype(jnp.float32)

    def places(index):
        body, vertex = index // verts, index % verts
        return [vertex % LANES, vertex // LANES, body]

    index = jnp.stack(places(pair_own[0]) + places(pair_far[0]) + [pair_own[0]] * 2, axis=0)
    full = jnp.pad(inverse, ((0, pad), (0, pad)))
    high = lax.reduce_precision(full, 8, 7)
    middle = (full - high).astype(jnp.bfloat16)
    high = high.astype(jnp.bfloat16)
    rest = to_rows(jnp.broadcast_to(rest_shape[:, None, :], positions.shape))
    dist = populations
    shape = to_rows(positions)
    for step_index in range(STEPS):
        density, momentum = moments(dist)
        flow = (momentum / density).reshape(3, lines, lanes)
        outgoing = jnp.einsum("cxl,lk->cxk", flow, cell_lane, precision=exact)
        outgoing = jnp.sum(outgoing * cell_line[None], axis=1)
        received = swap(outgoing)
        received = jnp.pad(received, ((0, 1), (0, 0)))
        vertex_flow = jnp.einsum("cs,bsv->bcv", received, slot_hot, precision=exact)
        predicted = shape + time_step * vertex_flow.reshape(shape.shape)
        shape = run_bodies(verts, shape, predicted, rest, high, middle, index)
        vertex_force = (coupling_gain * (shape - predicted)).reshape(bodies, BODY_ROWS, width)
        slot_force = jnp.einsum("bcv,bsv->cs", vertex_force, slot_hot, precision=exact)[:3]
        back = swap(slot_force)
        cell_force = jnp.einsum("cxk,lk->cxl", back[:, None, :] * cell_line[None], cell_lane, precision=exact)
        force = cell_force.reshape((3,) + grid_shape)
        dist = stream(collide(dist, force))
    return (dist, from_rows(shape))


def solution(mesh):
    placed = (
        P(None, "group", "brick", None),
        P(None, ("group", "brick"), None),
        P(),
        P(),
        P(("group", "brick"), None),
        P(("group", "brick"), None),
        P(("group", "brick"), None),
        P(("group", "brick"), None),
    )
    return jax.shard_map(
        on_device,
        mesh=mesh,
        in_specs=placed,
        out_specs=(P(None, "group", "brick", None), P(None, ("group", "brick"), None)),
        check_vma=False,
    )
```
